32 devices in a mesh: ka: 16 (over z, y, core), aux: 2 (over x).
Axes of the slice: x: 2, y: 2, z: 4, core: 2. Of those that a mesh axis runs over, the one named last changes fastest.
Arguments:
- coefficients: bfloat16 [16, 4096, 128], P('ka'), may hold values from -2.09375 to 2.09375
- triple: bfloat16 [64, 2, 64, 768], P('aux'), may hold values from -0.5 to 0.5
- neighbors: int32 [64, 2], P('aux'), may hold values from 0 to 63
- w_screened: bfloat16 [16, 768, 1536], P('ka', 'aux'), as said below
- partner: int32 [2, 16], replicated, may hold values from 0 to 15, each once within a row
- q_ids: int32 [2], replicated, may hold values from 0 to 15
Outputs:
- sigma: float32 [16, 64, 128], P('ka', 'aux')
The draws below stay inside these ranges and needn't reach their ends.
Inputs may be any that keep to these rules, and one draw needn't show every extreme that they name: Each stored w_screened is Hermitian: its real block is symmetric and its imaginary block antisymmetric.
All inputs are finite; a program needn't handle non-finite values.
Results may differ from the reference program's by a relative error of at most 0.0085.
Values may be sent and summed in bfloat16 or wider, within the bound.
A program may use at most 128 MiB of HBM per device.

```python
import math
import jax
import jax.numpy as jnp
from jax import lax

CELL_ATOMS = 64
ORBITALS_PER_ATOM = 64
AUX_ATOM = 12
SIGMA_BANDS = 64
OCCUPIED_BANDS = 16
NEIGH = 2
TRANSFERS = 2
ORB = 4096
NAUX = 768
NK = 16
QPTS = 16


def draw_w_screened(key, part):
    keys = jax.random.split(jax.random.fold_in(key, 31), QPTS)

    def single(subkey):
        first, second, third, fourth = jax.random.split(subkey, 4)
        sym_base = jax.random.normal(first, (NAUX, NAUX), jnp.float32)
        anti_base = jax.random.normal(second, (NAUX, NAUX), jnp.float32)
        magnitude = jax.random.uniform(third, (NAUX,), jnp.float32, 0.5, 1.5)
        signs = jnp.where(jax.random.bernoulli(fourth, 0.5, (NAUX,)), 1.0, -1.0)
        real_block = 0.6 * (sym_base + sym_base.T) / jnp.sqrt(2.0 * NAUX) + jnp.diag(magnitude * signs)
        imag_block = 0.6 * (anti_base - anti_base.T) / jnp.sqrt(2.0 * NAUX)
        return jnp.concatenate([real_block, imag_block], axis=1)
    return lax.map(single, keys).astype(jnp.bfloat16)


def with_ends(entries, rng, smallest, top_value):
    spot = [jax.random.randint(jax.random.fold_in(rng, axis), (), 0, length) for axis, length in enumerate(entries.shape)]
    longest = entries.shape.index(max(entries.shape))
    neighbour = spot[:longest] + [(spot[longest] + 1) % entries.shape[longest]] + spot[longest + 1:]
    return entries.at[tuple(spot)].set(smallest).at[tuple(neighbour)].set(top_value)


def levels(stream_key, extent, shards, smallest, largest):
    factor_of, own = 1.0, jax.random.fold_in(stream_key, 6)
    for axis_at, parts in shards:
        steps = jnp.exp(jax.random.uniform(jax.random.fold_in(own, axis_at), (parts,), jnp.float32, smallest / len(shards), largest / len(shards)))
        factor_of = factor_of * jnp.repeat(steps, extent[axis_at] // parts).reshape([-1 if axis == axis_at else 1 for axis in range(len(extent))])
    return factor_of


def bell_draw(stream_key, extent, deviation, most, pieces=(), kind=jnp.bfloat16):
    drawn = jax.random.normal(stream_key, extent, jnp.float32) * deviation
    if len(pieces) > 0:
        drawn = levels(stream_key, extent, pieces, -0.22, 0.18) * drawn
    return jnp.clip(drawn, min=-most, max=most).astype(kind)


def setup_inputs(seed: int = 0) -> dict:
    streams_of = jax.random.split(jax.random.key(seed), 7)
    coefficients = bell_draw(streams_of[0], (NK, ORB, 2 * SIGMA_BANDS), 0.35, 2.09375, ((0, 16),))
    triple = bell_draw(streams_of[1], (CELL_ATOMS, NEIGH, ORBITALS_PER_ATOM, AUX_ATOM * ORBITALS_PER_ATOM), (ORBITALS_PER_ATOM * NEIGH) ** -0.5, 0.5, ((0, 2),))
    neighbors = with_ends(jax.random.randint(streams_of[2], (CELL_ATOMS, NEIGH), 0, CELL_ATOMS), jax.random.fold_in(streams_of[2], 1), 0, CELL_ATOMS - 1).astype(jnp.int32)
    w_screened = draw_w_screened(jax.random.fold_in(streams_of[6], 71), 0)
    partner = jax.vmap(lambda own: jax.random.permutation(own, NK))(jax.random.split(streams_of[4], TRANSFERS)).reshape((TRANSFERS, NK)).astype(jnp.int32)
    q_ids = jax.random.randint(streams_of[5], (TRANSFERS,), 0, QPTS).astype(jnp.int32)
    return {"coefficients": coefficients, "triple": triple, "neighbors": neighbors, "w_screened": w_screened, "partner": partner, "q_ids": q_ids}


def reference(coefficients, triple, neighbors, w_screened, partner, q_ids):
    band_count = SIGMA_BANDS
    prefactor = -1.0 / math.sqrt(TRANSFERS * NAUX * OCCUPIED_BANDS)
    distant_coef_gathered = jnp.concatenate([coefficients[:, :, :OCCUPIED_BANDS], coefficients[:, :, SIGMA_BANDS:SIGMA_BANDS + OCCUPIED_BANDS]], axis=2)
    triple_wide = triple.astype(jnp.float32)

    def each_kpoint_values(kpoint_index):
        home_coefficients = coefficients[kpoint_index].reshape(CELL_ATOMS, ORBITALS_PER_ATOM, 2 * SIGMA_BANDS).astype(jnp.float32)
        blocks = jnp.zeros((2 * SIGMA_BANDS, 2 * SIGMA_BANDS), jnp.float32)
        for momentum_transfer in range(TRANSFERS):
            distant_coefficients = distant_coef_gathered[partner[momentum_transfer, kpoint_index]].reshape(CELL_ATOMS, ORBITALS_PER_ATOM, 2 * OCCUPIED_BANDS)
            neighbour_coef = jnp.take(distant_coefficients, neighbors, axis=0).astype(jnp.float32)
            pair_half = jnp.einsum('cjoy,cjox->cyx', neighbour_coef, triple_wide).astype(jnp.bfloat16)
            pair_half = pair_half.reshape(CELL_ATOMS, 2 * OCCUPIED_BANDS, AUX_ATOM, ORBITALS_PER_ATOM).astype(jnp.float32)
            combos = jnp.einsum('cix,cyai->cayx', home_coefficients, pair_half)
            real_part = combos[..., :OCCUPIED_BANDS, :band_count] + combos[..., OCCUPIED_BANDS:, band_count:]
            imag_part = combos[..., OCCUPIED_BANDS:, :band_count] - combos[..., :OCCUPIED_BANDS, band_count:]
            products = jnp.concatenate([real_part, imag_part], axis=-1).astype(jnp.bfloat16)
            products = products.reshape(NAUX, OCCUPIED_BANDS, 2 * SIGMA_BANDS)
            rotated = jnp.concatenate([-products[..., band_count:], products[..., :band_count]], axis=-1)
            stacked = jnp.concatenate([products, rotated], axis=0).reshape(2 * NAUX, OCCUPIED_BANDS * 2 * SIGMA_BANDS)
            weights = w_screened[q_ids[momentum_transfer]]
            screened = jnp.dot(weights, stacked, preferred_element_type=jnp.float32).astype(jnp.bfloat16)
            screened = screened.reshape(NAUX * OCCUPIED_BANDS, 2 * SIGMA_BANDS)
            left_side = products.reshape(NAUX * OCCUPIED_BANDS, 2 * SIGMA_BANDS)
            blocks = blocks + lax.dot_general(left_side, screened, (((0,), (0,)), ((), ())), preferred_element_type=jnp.float32)
        sigma_real = blocks[:band_count, :band_count] + blocks[band_count:, band_count:]
        sigma_imag = blocks[:band_count, band_count:] - blocks[band_count:, :band_count]
        return prefactor * jnp.concatenate([sigma_real, sigma_imag], axis=-1)
    return lax.map(each_kpoint_values, jnp.arange(NK, dtype=jnp.int32))
```

```python
import functools
import math

import jax
import jax.numpy as jnp
from jax import lax
from jax.experimental import pallas as pl
from jax.experimental.pallas import tpu as pltpu
from jax.sharding import PartitionSpec as P

AUX_ATOM = 12
OCC = 16
GROUP = 4
JOINED = 4
VMEM = pltpu.VMEM
SMEM = pltpu.SMEM
DMA = pltpu.SemaphoreType.DMA
MESH = pl.DeviceIdType.MESH


def bit_of(me, b):
    return lax.rem(lax.div(me, 1 << b), 2)


def flipped(me, b):
    return me + (1 << b) - 2 * (1 << b) * bit_of(me, b)


def down_rows(n, rows):
    sizes = [rows]
    for _ in range(1, n.bit_length() - 1):
        rows = rows // 2 if rows // 2 % 16 == 0 else rows
        sizes.append(rows)
    return sizes


def remote(src, dst, send, recv, device):
    return pltpu.make_async_remote_copy(
        src_ref=src, dst_ref=dst, send_sem=send, recv_sem=recv, device_id=device, device_id_type=MESH
    )


def pick_bands(coef, src):
    rows = src.shape[1]
    orbitals, doubled = coef.shape
    high = 2 * OCC
    band = lax.broadcasted_iota(jnp.int32, (high, doubled), 0)
    col = lax.broadcasted_iota(jnp.int32, (high, doubled), 1)
    want = jnp.where(band < OCC, band, band - OCC + doubled // 2)
    choose = jnp.where(col == want, 1.0, 0.0).astype(jnp.bfloat16)
    step = 8
    for p0 in range(0, orbitals // 128, step):
        wide = lax.dot_general(
            choose,
            coef[p0 * 128 : (p0 + step) * 128, :],
            (((1,), (1,)), ((), ())),
            preferred_element_type=jnp.float32,
        ).astype(jnp.bfloat16)
        for p in range(p0, p0 + step):
            block = wide[:, (p - p0) * 128 : (p - p0 + 1) * 128]
            if rows >= high:
                at = p * high % rows
                src[p * high // rows, at : at + high, :] = block
            else:
                for i in range(high // rows):
                    src[p * (high // rows) + i] = block[i * rows : (i + 1) * rows]


def mask_weights(me, half, q_ref, w, kept, sent):
    size = w.shape[0]
    naux = w.shape[1] // 2
    own = pl.multiple_of(half * size, 128)
    other = pl.multiple_of((1 - half) * size, 128)
    first = me == q_ref[half]
    second = me == q_ref[1 - half]
    low = bit_of(me, 0) == 0
    tile = 64
    for r in range(0, size, tile):
        span = slice(r, r + tile)
        row = lax.broadcasted_iota(jnp.int32, (tile, size), 0) + r
        col = lax.broadcasted_iota(jnp.int32, (tile, size), 1)
        packed = jnp.where(
            row <= col,
            w[span, pl.ds(own, size)].astype(jnp.float32),
            w[span, pl.ds(own + naux, size)].astype(jnp.float32),
        ).astype(jnp.bfloat16)
        zero = jnp.zeros_like(packed)
        pieces = [
            jnp.where(first, packed, zero),
            jnp.where(first, w[span, pl.ds(other, size)], zero),
            jnp.where(second, packed, zero),
            jnp.where(first, w[span, pl.ds(other + naux, size)], zero),
        ]
        for i in range(2):
            at = slice(i * size + r, i * size + r + tile)
            kept[at] = jnp.where(low, pieces[i], pieces[2 + i])
            sent[at] = jnp.where(low, pieces[2 + i], pieces[i])


def place_far(t, transfers, landed, far):
    rows = landed.shape[2]
    high = 2 * OCC
    for p in range(far.shape[1]):
        if rows >= high:
            at = p * high % rows
            block = landed[t, p * high // rows, at : at + high, :]
        else:
            block = jnp.concatenate(
                [landed[t, p * (high // rows) + i] for i in range(high // rows)], axis=0
            )
        turned = pltpu.roll(block.astype(jnp.float32), 64, 1).astype(jnp.bfloat16)
        for r in range(2):
            at = (r * transfers + t) * OCC
            far[0, p, at : at + OCC, :] = block[r * OCC : (r + 1) * OCC]
            far[1, p, at : at + OCC, :] = turned[r * OCC : (r + 1) * OCC]


def pair_group(i, first_atom, nb_ref, far, triple, coef, own, part, stage):
    low = lax.broadcasted_iota(jnp.int32, (4 * OCC, 128), 1) < 64
    sign = jnp.where(lax.broadcasted_iota(jnp.int32, (64, 128), 1) < 64, 1.0, -1.0)
    zero = jnp.zeros((64, 128), jnp.bfloat16)
    for g in range(GROUP):
        c = i * GROUP + g
        n0 = nb_ref[0, c]
        n1 = nb_ref[1, c]
        x0 = far[lax.rem(n0, 2), lax.div(n0, 2)]
        x1 = far[1 - lax.rem(n1, 2), lax.div(n1, 2)]
        lhs = jnp.where(low, x0, x1)
        half = jnp.dot(lhs, triple[c], preferred_element_type=jnp.float32)
        half = half.astype(jnp.bfloat16)
        top, bottom = half[: 2 * OCC], half[2 * OCC :]
        at = pl.multiple_of((first_atom + c) * 64, 64)
        home = coef[pl.ds(at, 64), :].astype(jnp.float32)
        with_real = (home * sign).astype(jnp.bfloat16)
        with_imag = pltpu.roll(home, 64, 1).astype(jnp.bfloat16)
        rhs = jnp.concatenate(
            [
                jnp.concatenate([with_real, zero], axis=1),
                jnp.concatenate([zero, with_real], axis=1),
                jnp.concatenate([with_imag, zero], axis=1),
                jnp.concatenate([zero, with_imag], axis=1),
            ],
            axis=0,
        )
        rows = jnp.concatenate(
            [
                jnp.concatenate(
                    [top[:, s * 128 : (s + 1) * 128], bottom[:, s * 128 : (s + 1) * 128]], axis=1
                )
                for s in range(AUX_ATOM // 2)
            ],
            axis=0,
        )
        prod = jnp.dot(rows, rhs, preferred_element_type=jnp.float32)
        for s in range(AUX_ATOM // 2):
            for t in range(2):
                for b in range(2):
                    at = (g * AUX_ATOM + 2 * s + b) * OCC
                    r = s * 2 * OCC + t * OCC
                    stage[t, at : at + OCC, :] = prod[r : r + OCC, b * 128 : (b + 1) * 128]
    count = GROUP * AUX_ATOM
    for t, out in enumerate((own, part)):
        for l in range(OCC):
            out[i, l] = stage[t, pl.ds(l, count, stride=OCC), :].astype(jnp.bfloat16)


def unpack_weights(full, first, second, cross):
    size = first.shape[1]
    row = lax.broadcasted_iota(jnp.int32, (size, size), 0)
    col = lax.broadcasted_iota(jnp.int32, (size, size), 1)
    for piece, out in ((0, first), (2, second)):
        packed = full[piece * size : (piece + 1) * size].astype(jnp.float32)
        turned = packed.T
        out[:size] = jnp.where(row <= col, packed, turned).astype(jnp.bfloat16)
        signed = jnp.where(row > col, packed, -turned)
        out[size:] = jnp.where(row == col, 0.0, signed).astype(jnp.bfloat16)
    for i, piece in enumerate((1, 3)):
        block = full[piece * size : (piece + 1) * size].astype(jnp.float32)
        cross[i * size : (i + 1) * size] = block.T.astype(jnp.bfloat16)


def screen_bands(e, own, part, first, second, cross, zbuf, total):
    blocks, _, count, doubled = own.shape
    size = blocks * count
    sign = jnp.where(lax.broadcasted_iota(jnp.int32, (size, doubled), 1) < doubled // 2, -1.0, 1.0)

    def columns(x):
        return [
            jnp.concatenate([x[c, e * JOINED + i] for c in range(blocks)], axis=0)
            for i in range(JOINED)
        ]

    def apply(weights, wide, conj):
        prod = jnp.dot(weights[...], wide, preferred_element_type=jnp.float32)
        result = []
        for i in range(JOINED):
            re = prod[:size, i * doubled : (i + 1) * doubled]
            im = sign * pltpu.roll(prod[size:, i * doubled : (i + 1) * doubled], doubled // 2, 1)
            result.append((re - im if conj else re + im).astype(jnp.bfloat16))
        return result

    mine = columns(own)
    wide = jnp.concatenate(mine, axis=1)
    lefts = list(mine)
    screened = apply(first, wide, False)
    for i, z in enumerate(apply(cross, wide, True)):
        for c in range(blocks):
            zbuf[c, e * JOINED + i] = z[c * count : (c + 1) * count]
    theirs = columns(part)
    lefts += theirs
    screened += apply(second, jnp.concatenate(theirs, axis=1), False)
    total[...] += lax.dot_general(
        jnp.concatenate(lefts, axis=0),
        jnp.concatenate(screened, axis=0),
        (((0,), (0,)), ((), ())),
        preferred_element_type=jnp.float32,
    )


def sigma_kernel(
    n, prefactor, partner_ref, q_ref, nb_ref, coef_in, triple_in, w_in, out_ref,
    coef, triple, w, src, spread, picked, landed, far,
    kept, sent, accs, recvs, full, first, second, cross,
    own, part, incoming, zbuf, stage, total, give, got,
    local_sem, triple_sem, s1, r1, s2, r2, sw, rw, su, ru, sc, rc, sf, rf,
):
    me = lax.axis_index("ka")
    half = lax.axis_index("aux")
    transfers = partner_ref.shape[0]
    atoms = triple.shape[0]
    blocks = own.shape[0]
    bits = n.bit_length() - 1
    barrier = pltpu.get_barrier_semaphore()

    def greet(off, carry):
        dst = lax.rem(me + off, n)
        pl.semaphore_signal(barrier, inc=1, device_id={"ka": dst}, device_id_type=MESH)
        return carry

    lax.fori_loop(1, n, greet, 0)
    pl.semaphore_signal(barrier, inc=1, device_id={"aux": 1 - half}, device_id_type=MESH)

    get_coef = pltpu.make_async_copy(coef_in, coef, local_sem.at[0])
    get_w = pltpu.make_async_copy(w_in, w, local_sem.at[1])
    get_coef.start()
    get_w.start()

    def get_triple(i):
        span = pl.ds(i * GROUP, GROUP)
        return pltpu.make_async_copy(triple_in.at[span], triple.at[span], triple_sem.at[i])

    for i in range(blocks):
        get_triple(i).start()
    get_coef.wait()
    pick_bands(coef, src)
    pl.semaphore_wait(barrier, n)

    def over_peers(act):
        def body(off, carry):
            act(off, lax.rem(me + off, n))
            return carry

        lax.fori_loop(1, n, body, 0)

    def spread_copy(off, dst):
        return remote(src.at[dst], spread.at[me], s1.at[off], r1.at[off], {"ka": dst})

    def return_copy(t, off, dst):
        return remote(picked.at[t, dst], landed.at[t, me], s2.at[t, off], r2.at[t, off], {"ka": dst})

    over_peers(lambda off, dst: spread_copy(off, dst).start())
    spread[me] = src[me]

    sizes = down_rows(n, kept.shape[0])
    halved = [b == 0 or sizes[b] < sizes[b - 1] for b in range(bits)]
    starts, at = [], 0
    for b in range(bits):
        if halved[b]:
            at = at + bit_of(me, b) * sizes[b]
        starts.append(at)

    def down_copy(b):
        if b == 0:
            out = sent
        elif halved[b]:
            far_half = pl.multiple_of((1 - bit_of(me, b)) * sizes[b], 16)
            out = accs[b - 1].at[pl.ds(far_half, sizes[b])]
        else:
            out = accs[b - 1]
        return remote(out, recvs[b], sw.at[b], rw.at[b], {"ka": flipped(me, b)})

    def down_finish(b):
        down_copy(b).wait()
        if b == 0:
            mine = kept[...]
        elif halved[b]:
            near = pl.multiple_of(bit_of(me, b) * sizes[b], 16)
            mine = accs[b - 1][pl.ds(near, sizes[b])]
        else:
            mine = accs[b - 1][...]
        summed = mine + recvs[b][...]
        if b == bits - 1:
            full[pl.ds(pl.multiple_of(starts[b], 16), sizes[b])] = summed
        else:
            accs[b][...] = summed
            down_copy(b + 1).start()

    up_order = [b for b in reversed(range(bits)) if halved[b]]

    def up_copy(b):
        span = pl.ds(pl.multiple_of(starts[b], 16), sizes[b])
        return remote(full.at[span], full.at[span], su.at[b], ru.at[b], {"ka": flipped(me, b)})

    get_w.wait()
    mask_weights(me, half, q_ref, w, kept, sent)
    down_copy(0).start()
    down_finish(0)

    over_peers(lambda off, dst: spread_copy(off, dst).wait())
    for t in reversed(range(transfers)):
        which = lax.rem(half + t, transfers)

        def pick(k, carry, t=t, which=which):
            picked[t, k] = spread[partner_ref[which, k]]
            return carry

        lax.fori_loop(0, n, pick, 0)
        over_peers(lambda off, dst, t=t: return_copy(t, off, dst).start())
        landed[t, me] = picked[t, me]
    down_finish(1)
    for t in reversed(range(transfers)):
        over_peers(lambda off, dst, t=t: return_copy(t, off, dst).wait())
        place_far(t, transfers, landed, far)

    def cross_copy(i):
        return remote(part.at[i], incoming.at[i], sc.at[i], rc.at[i], {"aux": 1 - half})

    def pair(i, carry):
        get_triple(i).wait()
        pair_group(i, half * atoms, nb_ref, far, triple, coef, own, part, stage)
        cross_copy(i).start()
        return carry

    lax.fori_loop(0, blocks, pair, 0)
    for b in range(2, bits):
        down_finish(b)
    for b in up_order:
        up_copy(b).start()
        up_copy(b).wait()
    unpack_weights(full, first, second, cross)
    total[...] = jnp.zeros_like(total)

    def screen(e, carry):
        screen_bands(e, own, part, first, second, cross, zbuf, total)
        return carry

    lax.fori_loop(0, OCC // JOINED, screen, 0)
    total[...] = 0.5 * total[...]

    def meet(i, carry):
        cross_copy(i).wait()
        count = own.shape[2]
        total[...] += lax.dot_general(
            zbuf[i].reshape(OCC * count, 128),
            incoming[i].reshape(OCC * count, 128),
            (((0,), (0,)), ((), ())),
            preferred_element_type=jnp.float32,
        )
        return carry

    lax.fori_loop(0, blocks, meet, 0)
    value = total[...]
    bands = value.shape[0] // 2
    real = value[:bands, :bands] + value[bands:, bands:]
    imag = value[:bands, bands:] - value[bands:, :bands]
    sigma = prefactor * jnp.concatenate([real + real.T, imag - imag.T], axis=1)
    top, bottom = sigma[: bands // 2], sigma[bands // 2 :]
    low = half == 0
    give[...] = jnp.where(low, bottom, top)
    last = remote(give, got, sf.at[0], rf.at[0], {"aux": 1 - half})
    last.start()
    mine = jnp.where(low, top, bottom)
    last.wait()
    out_ref[...] = mine + got[...]


def local(n, coefficients, triple, neighbors, w_screened, partner, q_ids):
    transfers = partner.shape[0]
    coef = coefficients[0]
    orbitals, doubled = coef.shape
    atoms, neigh, per_atom, width = triple.shape
    size = w_screened.shape[1]
    naux = w_screened.shape[2] // 2
    prefactor = -1.0 / math.sqrt(transfers * naux * OCC)
    bits = n.bit_length() - 1
    blocks = atoms // GROUP
    pairs = orbitals // 128
    bf16 = jnp.bfloat16
    block = (n, pairs * 2 * OCC // n, 128)
    sizes = down_rows(n, 2 * size)
    chunk = (blocks, OCC, GROUP * AUX_ATOM, doubled)
    wide = (2 * size, size)
    scratch = [
        VMEM(coef.shape, bf16),
        VMEM((atoms, neigh * per_atom, width), bf16),
        VMEM(w_screened.shape[1:], bf16),
        VMEM(block, bf16),
        VMEM(block, bf16),
        VMEM((transfers,) + block, bf16),
        VMEM((transfers,) + block, bf16),
        VMEM((2, pairs, 2 * transfers * OCC, 128), bf16),
        VMEM(wide, bf16),
        VMEM(wide, bf16),
        [VMEM((rows, size), bf16) for rows in sizes[:-1]],
        [VMEM((rows, size), bf16) for rows in sizes],
        VMEM((4 * size, size), bf16),
        VMEM(wide, bf16),
        VMEM(wide, bf16),
        VMEM(wide, bf16),
        VMEM(chunk, bf16),
        VMEM(chunk, bf16),
        VMEM(chunk, bf16),
        VMEM(chunk, bf16),
        VMEM((2, GROUP * AUX_ATOM * OCC, 128), jnp.float32),
        VMEM((doubled, doubled), jnp.float32),
        VMEM((doubled // 4, doubled), jnp.float32),
        VMEM((doubled // 4, doubled), jnp.float32),
        DMA((2,)),
        DMA((blocks,)),
        DMA((n,)),
        DMA((n,)),
        DMA((transfers, n)),
        DMA((transfers, n)),
        DMA((bits,)),
        DMA((bits,)),
        DMA((bits,)),
        DMA((bits,)),
        DMA((blocks,)),
        DMA((blocks,)),
        DMA((1,)),
        DMA((1,)),
    ]
    any_spec = pl.BlockSpec(memory_space=pl.ANY)
    smem_spec = pl.BlockSpec(memory_space=SMEM)
    result = pl.pallas_call(
        functools.partial(sigma_kernel, n, prefactor),
        out_shape=jax.ShapeDtypeStruct((doubled // 4, doubled), jnp.float32),
        in_specs=[smem_spec] * 3 + [any_spec] * 3,
        out_specs=pl.BlockSpec(memory_space=VMEM),
        scratch_shapes=scratch,
        compiler_params=pltpu.CompilerParams(collective_id=0, has_side_effects=True),
        name="sigma",
    )(
        partner,
        q_ids,
        neighbors.T,
        coef,
        triple.reshape(atoms, neigh * per_atom, width),
        w_screened[0],
    )
    return result[None]


def solution(mesh):
    in_specs = (
        P("ka", None, None),
        P("aux", None, None, None),
        P("aux", None),
        P("ka", "aux", None),
        P(),
        P(),
    )
    return jax.shard_map(
        functools.partial(local, mesh.shape["ka"]),
        mesh=mesh,
        in_specs=in_specs,
        out_specs=P("ka", "aux", None),
        check_vma=False,
    )
```

```python
import functools
import math

import jax
import jax.numpy as jnp
from jax import lax
from jax.experimental import pallas as pl
from jax.experimental.pallas import tpu as pltpu
from jax.sharding import PartitionSpec as P

AUX_ATOM = 12
OCC = 16
GROUP = 4
JOINED = 4
SHARE = ((1, 2), (2, 1), (1, 2))
EARLY = 3
ORDER = (
    "first0", "first1", "spread", "back", "second0", "second1", "relay00", "far0", "middle1",
    "middle0", "far1", "relay20", "relay10", "swap0", "turn1", "swap1", "pair0", "pair1", "turn0",
    "relay11", "pair2", "pair3", "up1", "up0", "relay01", "pair4", "pair5", "pair6", "pair7",
    "rest1", "rest0", "relay21", "relay12", "relay02", "done1", "done0", "screen", "relay22",
    "names", "other0", "other1", "other2",
)
VMEM = pltpu.VMEM
SMEM = pltpu.SMEM
DMA = pltpu.SemaphoreType.DMA
MESH = pl.DeviceIdType.MESH


def bit_of(me, b):
    return lax.rem(lax.div(me, 1 << b), 2)


def flipped(me, b):
    return me + (1 << b) - 2 * (1 << b) * bit_of(me, b)


def down_rows(n, rows):
    sizes = []
    bits = n.bit_length() - 1
    for b in range(bits):
        rows = rows // 2 if rows // 2 % 16 == 0 and b < bits - 1 else rows
        sizes.append(rows)
    return sizes


class Lane:
    def __init__(self, me, order, sent, kept, full, accs, recvs, sems):
        self.me, self.order = me, order
        self.sent, self.kept, self.full, self.accs, self.recvs = sent, kept, full, accs, recvs
        self.sizes = [x.shape[0] for x in recvs]
        rows = full.shape[0]
        self.halved, self.starts, at = [], [], 0
        for b, size in zip(order, self.sizes):
            self.halved.append(size < rows)
            if size < rows:
                at = at + bit_of(me, b) * size
            self.starts.append(pl.multiple_of(at, 16))
            rows = size
        self.down_send, self.down_recv, self.up_send, self.up_recv = sems

    def peer(self, s):
        return {"ka": flipped(self.me, self.order[s])}

    def down(self, s):
        if s == 0:
            out = self.sent
        elif self.halved[s]:
            away = pl.multiple_of((1 - bit_of(self.me, self.order[s])) * self.sizes[s], 16)
            out = self.accs[s - 1].at[pl.ds(away, self.sizes[s])]
        else:
            out = self.accs[s - 1]
        return remote(out, self.recvs[s], self.down_send.at[s], self.down_recv.at[s], self.peer(s))

    def step(self, s):
        self.down(s).wait()
        if s == 0:
            mine = self.kept[...]
        elif self.halved[s]:
            near = pl.multiple_of(bit_of(self.me, self.order[s]) * self.sizes[s], 16)
            mine = self.accs[s - 1][pl.ds(near, self.sizes[s])]
        else:
            mine = self.accs[s - 1][...]
        summed = mine + self.recvs[s][...]
        if s == len(self.order) - 1:
            self.full[pl.ds(self.starts[s], self.sizes[s])] = summed
        else:
            self.accs[s][...] = summed
            self.down(s + 1).start()

    def up(self, s):
        span = pl.ds(self.starts[s], self.sizes[s])
        return remote(
            self.full.at[span], self.full.at[span], self.up_send.at[s], self.up_recv.at[s], self.peer(s)
        )


def remote(src, dst, send, recv, device):
    return pltpu.make_async_remote_copy(
        src_ref=src, dst_ref=dst, send_sem=send, recv_sem=recv, device_id=device, device_id_type=MESH
    )


def pick_bands(first, coef, src):
    rows = src.shape[1]
    doubled = coef.shape[1]
    high = 2 * OCC
    pairs = src.shape[0] * rows // high
    band = lax.broadcasted_iota(jnp.int32, (high, doubled), 0)
    col = lax.broadcasted_iota(jnp.int32, (high, doubled), 1)
    want = jnp.where(band < OCC, band, band - OCC + doubled // 2)
    choose = jnp.where(col == want, 1.0, 0.0).astype(jnp.bfloat16)
    step = min(8, pairs)
    for p0 in range(0, pairs, step):
        wide = lax.dot_general(
            choose,
            coef[pl.ds(pl.multiple_of(first + p0 * 128, 128), step * 128), :],
            (((1,), (1,)), ((), ())),
            preferred_element_type=jnp.float32,
        ).astype(jnp.bfloat16)
        for p in range(p0, p0 + step):
            block = wide[:, (p - p0) * 128 : (p - p0 + 1) * 128]
            if rows >= high:
                at = p * high % rows
                src[p * high // rows, at : at + high, :] = block
            else:
                for i in range(high // rows):
                    src[p * (high // rows) + i] = block[i * rows : (i + 1) * rows]


def mask_weights(me, half, q_ref, w, kept, sent):
    size = w.shape[0]
    naux = w.shape[1] // 2
    own = pl.multiple_of(half * size, 128)
    other = pl.multiple_of((1 - half) * size, 128)
    first = me == q_ref[half]
    second = me == q_ref[1 - half]
    low = bit_of(me, 0) == 0
    tile = 64
    for r in range(0, size, tile):
        span = slice(r, r + tile)
        row = lax.broadcasted_iota(jnp.int32, (tile, size), 0) + r
        col = lax.broadcasted_iota(jnp.int32, (tile, size), 1)
        packed = jnp.where(
            row <= col,
            w[span, pl.ds(own, size)].astype(jnp.float32),
            w[span, pl.ds(own + naux, size)].astype(jnp.float32),
        ).astype(jnp.bfloat16)
        zero = jnp.zeros_like(packed)
        pieces = [
            jnp.where(first, packed, zero),
            jnp.where(second, packed, zero),
            jnp.where(first, w[span, pl.ds(other, size)], zero),
            jnp.where(first, w[span, pl.ds(other + naux, size)], zero),
        ]
        for i in range(2):
            lower, upper = pieces[2 * i : 2 * i + 2]
            kept[i][span] = jnp.where(low, lower, upper)
            sent[i][span] = jnp.where(low, upper, lower)


def place_far(t, transfers, first, landed, far):
    rows = landed.shape[1]
    high = 2 * OCC
    for p in range(landed.shape[0] * rows // high):
        if rows >= high:
            at = p * high % rows
            block = landed[p * high // rows, at : at + high, :]
        else:
            block = jnp.concatenate(
                [landed[p * (high // rows) + i] for i in range(high // rows)], axis=0
            )
        turned = pltpu.roll(block.astype(jnp.float32), 64, 1).astype(jnp.bfloat16)
        for r in range(2):
            at = pl.multiple_of((r * transfers + t) * OCC, OCC)
            far[0, first + p, pl.ds(at, OCC), :] = block[r * OCC : (r + 1) * OCC]
            far[1, first + p, pl.ds(at, OCC), :] = turned[r * OCC : (r + 1) * OCC]


def pair_group(first_atom, nb_ref, far, triple, coef, outs, stage):
    low = lax.broadcasted_iota(jnp.int32, (4 * OCC, 128), 1) < 64
    sign = jnp.where(lax.broadcasted_iota(jnp.int32, (64, 128), 1) < 64, 1.0, -1.0)
    zero = jnp.zeros((64, 128), jnp.bfloat16)
    for g in range(GROUP):
        n0 = nb_ref(0, g)
        n1 = nb_ref(1, g)
        x0 = far[lax.rem(n0, 2), lax.div(n0, 2)]
        x1 = far[1 - lax.rem(n1, 2), lax.div(n1, 2)]
        lhs = jnp.where(low, x0, x1)
        half = jnp.dot(lhs, triple(g), preferred_element_type=jnp.float32)
        half = half.astype(jnp.bfloat16)
        top, bottom = half[: 2 * OCC], half[2 * OCC :]
        at = pl.multiple_of((first_atom + g) * 64, 64)
        home = coef[pl.ds(at, 64), :].astype(jnp.float32)
        with_real = (home * sign).astype(jnp.bfloat16)
        with_imag = pltpu.roll(home, 64, 1).astype(jnp.bfloat16)
        rhs = jnp.concatenate(
            [
                jnp.concatenate([with_real, zero], axis=1),
                jnp.concatenate([zero, with_real], axis=1),
                jnp.concatenate([with_imag, zero], axis=1),
                jnp.concatenate([zero, with_imag], axis=1),
            ],
            axis=0,
        )
        rows = jnp.concatenate(
            [
                jnp.concatenate(
                    [top[:, s * 128 : (s + 1) * 128], bottom[:, s * 128 : (s + 1) * 128]], axis=1
                )
                for s in range(AUX_ATOM // 2)
            ],
            axis=0,
        )
        prod = jnp.dot(rows, rhs, preferred_element_type=jnp.float32)
        for s in range(AUX_ATOM // 2):
            for t in outs:
                for b in range(2):
                    at = (g * AUX_ATOM + 2 * s + b) * OCC
                    r = s * 2 * OCC + t * OCC
                    stage[t, at : at + OCC, :] = prod[r : r + OCC, b * 128 : (b + 1) * 128]
    count = GROUP * AUX_ATOM
    for t, out in outs.items():
        for l in range(OCC):
            out[l] = stage[t, pl.ds(l, count, stride=OCC), :].astype(jnp.bfloat16)


def unpack_diagonal(packed, upper, lower):
    size = packed.shape[1]
    cut = upper.shape[0] // 2
    row = lax.broadcasted_iota(jnp.int32, (size, size), 0)
    col = lax.broadcasted_iota(jnp.int32, (size, size), 1)
    value = packed.astype(jnp.float32)
    turned = value.T
    real = jnp.where(row <= col, value, turned)
    imag = jnp.where(row > col, value, -turned)
    imag = jnp.where(row == col, 0.0, imag)
    twice = jnp.where(lax.broadcasted_iota(jnp.int32, (cut, size), 1) < cut, 1.0, 2.0)
    upper[:cut] = (twice * real[:cut]).astype(jnp.bfloat16)
    upper[cut:] = (twice * imag[:cut]).astype(jnp.bfloat16)
    lower[: size - cut] = real[cut:, cut:].astype(jnp.bfloat16)
    lower[size - cut :] = imag[cut:, cut:].astype(jnp.bfloat16)


def unpack_cross(full, cross):
    size = full.shape[1]
    for i in range(2):
        span = slice(i * size, (i + 1) * size)
        cross[span] = full[span].astype(jnp.float32).T.astype(jnp.bfloat16)


def columns(x, e):
    return [
        jnp.concatenate([x[c, e * JOINED + i] for c in range(x.shape[0])], axis=0)
        for i in range(JOINED)
    ]


def apply(weights, wide, conj):
    size = weights.shape[0] // 2
    sign = jnp.where(lax.broadcasted_iota(jnp.int32, (size, 128), 1) < 64, -1.0, 1.0)
    prod = jnp.dot(weights[...], wide, preferred_element_type=jnp.float32)
    result = []
    for i in range(JOINED):
        re = prod[:size, i * 128 : (i + 1) * 128]
        im = sign * pltpu.roll(prod[size:, i * 128 : (i + 1) * 128], 64, 1)
        result.append((re - im if conj else re + im).astype(jnp.bfloat16))
    return result


def gram(left, right):
    return lax.dot_general(left, right, (((0,), (0,)), ((), ())), preferred_element_type=jnp.float32)


def diagonal(parts, upper, lower):
    cut = upper.shape[0] // 2
    wide = jnp.concatenate(parts, axis=1)
    first = apply(upper, wide, False)
    rest = apply(lower, wide[cut:], False)
    return [part for both in zip(first, rest) for part in both]


def screen_bands(e, own, part, uppers, lowers, cross, zbuf, total):
    count = own.shape[2]
    mine = columns(own, e)
    for i, z in enumerate(apply(cross, jnp.concatenate(mine, axis=1), True)):
        for c in range(own.shape[0]):
            zbuf[c, e * JOINED + i] = z[c * count : (c + 1) * count]
    theirs = columns(part, e)
    screened = diagonal(mine, uppers[0], lowers[0]) + diagonal(theirs, uppers[1], lowers[1])
    total[...] += gram(jnp.concatenate(mine + theirs, axis=0), jnp.concatenate(screened, axis=0))


def sigma_kernel(
    n, prefactor, partner_ref, q_ref, nb_ref, nb_in, coef_in, triple_in, w_in, out_ref,
    coef, triple, w, src, spread, picked, landed, swapped, far,
    kept, sent, accs, recvs, full, uppers, lowers, cross,
    own, part, incoming, zbuf, stage, total, give, got, other, nb_land, nb_other,
    local_sem, triple_sem, s1, r1, s2, r2, s3, r3, lane_sems, sc, rc, sf, rf, fetch_sems,
):
    me = lax.axis_index("ka")
    half = lax.axis_index("aux")
    transfers = partner_ref.shape[0]
    atoms = triple.shape[0] // 2
    group_rows = 2 * GROUP
    blocks = own.shape[0]
    fetched = len(SHARE)
    crossing = blocks - fetched
    bits = n.bit_length() - 1
    across = {"aux": 1 - half}
    barrier = pltpu.get_barrier_semaphore()

    def greet(off, carry):
        dst = lax.rem(me + off, n)
        pl.semaphore_signal(barrier, inc=1, device_id={"ka": dst}, device_id_type=MESH)
        return carry

    lax.fori_loop(1, n, greet, 0)
    pl.semaphore_signal(barrier, inc=1, device_id=across, device_id_type=MESH)

    def get_coef(near):
        rows = coef.shape[0] // 2
        span = pl.ds(pl.multiple_of((half if near else 1 - half) * rows, 128), rows)
        return pltpu.make_async_copy(coef_in.at[span], coef.at[span], local_sem.at[0 if near else 2])

    get_w = pltpu.make_async_copy(w_in, w, local_sem.at[1])
    get_coef(True).start()
    get_w.start()

    def get_triple(i):
        span = pl.ds(i * group_rows, group_rows)
        return pltpu.make_async_copy(triple_in.at[span], triple.at[span], triple_sem.at[i])

    def over_peers(act):
        def body(off, carry):
            act(off, lax.rem(me + off, n))
            return carry

        lax.fori_loop(1, n, body, 0)

    def spread_copy(off, dst):
        return remote(src.at[dst], spread.at[me], s1.at[off], r1.at[off], {"ka": dst})

    def return_copy(t, off, dst):
        return remote(picked.at[t, dst], landed.at[t, me], s2.at[t, off], r2.at[t, off], {"ka": dst})

    core = bit_of(me, 0)
    nb_copy = remote(nb_in, nb_land, sf.at[1], rf.at[1], across)

    def swap(t):
        return remote(landed.at[t], swapped.at[t], s3.at[t], r3.at[t], across)

    def piece(i, level):
        bits_of = SHARE[i] + (0,)
        size = group_rows >> len(bits_of)
        at = 0
        for j in range(level, len(bits_of)):
            at = at + (size << j) * bit_of(me, bits_of[j])
        return at, size << level

    def fetch(i):
        at, size = piece(i, 0)
        return remote(
            triple_in.at[pl.ds((crossing + i) * group_rows + at, size)],
            other.at[i, pl.ds(at, size)],
            fetch_sems[0].at[i],
            fetch_sems[1].at[i],
            across,
        )

    def pass_on(i, level):
        at, size = piece(i, level)
        span = other.at[i, pl.ds(at, size)]
        peer = {"ka": flipped(me, (SHARE[i] + (0,))[level])}
        return remote(span, span, fetch_sems[2].at[i, level], fetch_sems[3].at[i, level], peer)

    def relay(i, level):
        if level == 0:
            fetch(i).wait()
        else:
            pass_on(i, level - 1).wait()
        pass_on(i, level).start()

    lanes = [
        Lane(me, order, sent[i], kept[i], full[i], accs[i], recvs[i], lane_sems[i])
        for i, order in enumerate(lane_orders(bits))
    ]

    tops = [s for s in reversed(range(bits)) if lanes[0].halved[s]]

    def raise_lane(lane, i):
        if i > 0:
            lane.up(tops[i - 1]).wait()
        if i < len(tops):
            lane.up(tops[i]).start()

    def cross_copy(i):
        return remote(part.at[i], incoming.at[i], sc.at[i], rc.at[i], across)

    def pair(i, outs):
        pair_group(
            half * atoms + i * GROUP,
            lambda j, g: nb_ref[j, i * GROUP + g],
            far,
            lambda g: triple[pl.ds((i * GROUP + g) * 2, 2)].reshape(128, triple.shape[2]),
            coef,
            outs,
            stage,
        )

    def pair_mine(i):
        get_triple(i).wait()
        pair(i, {0: own.at[i], 1: part.at[i]})
        if i < crossing:
            cross_copy(i).start()

    def pair_other(i):
        pass_on(i, len(SHARE[i])).wait()
        pair_group(
            (1 - half) * atoms + (crossing + i) * GROUP,
            lambda j, g: nb_other[j, (crossing + i) * GROUP + g],
            far,
            lambda g: other[i, 2 * g : 2 * g + 2].reshape(128, triple.shape[2]),
            coef,
            {0: incoming.at[crossing + i]},
            stage,
        )

    def send_back(t):
        over_peers(lambda off, dst: return_copy(t, off, dst).start())

    get_coef(True).wait()
    pick_bands(half * (coef.shape[0] // 2), coef, src)
    get_w.wait()
    mask_weights(me, half, q_ref, w, kept, sent)
    pl.semaphore_wait(barrier, n)
    over_peers(lambda off, dst: spread_copy(off, dst).start())
    for lane in lanes:
        lane.down(0).start()
    nb_copy.start()
    for i in range(EARLY):
        fetch(i).start()
    spread[me] = src[me]
    get_coef(False).start()
    for i in range(blocks):
        get_triple(i).start()

    def pick(t):
        def body(k, carry):
            picked[t, k] = spread[partner_ref[t, k]]
            return carry

        lax.fori_loop(0, n, body, 0)
        landed[t, me] = picked[t, me]

    def spread_done():
        over_peers(lambda off, dst: spread_copy(off, dst).wait())
        for t in range(transfers):
            pick(t)
            if t == 0:
                send_back(t)

    far_half = far.shape[1] // 2

    def returned(t):
        over_peers(lambda off, dst: return_copy(t, off, dst).wait())
        swap(t).start()
        place_far(lax.rem(half + t, 2), transfers, half * far_half, landed.at[t], far)

    def exchanged(t):
        swap(t).wait()
        place_far(lax.rem(half + t, 2), transfers, (1 - half) * far_half, swapped.at[t], far)

    def fetch_rest():
        for i in range(EARLY, fetched):
            fetch(i).start()

    def middle(lane):
        for s in range(2, bits - 1):
            lane.step(s)

    def last_down(lane):
        lane.step(bits - 1)
        raise_lane(lane, 0)

    def rest_up(lane):
        for i in range(2, len(tops)):
            raise_lane(lane, i)

    def names_done():
        get_coef(False).wait()
        nb_copy.wait()
        move = pltpu.make_async_copy(nb_land, nb_other, local_sem.at[3])
        move.start()
        move.wait()

    def lane_done(i):
        raise_lane(lanes[i], len(tops))
        if i == 0:
            size = cross.shape[1]
            for j in range(2):
                unpack_diagonal(full[0][j * size : (j + 1) * size], uppers[j], lowers[j])
        else:
            unpack_cross(full[1], cross)

    def loop(start, stop, body):
        lax.fori_loop(start, stop, body, 0)

    def screen(e, carry):
        screen_bands(e, own, part, uppers, lowers, cross, zbuf, total)
        return carry

    steps = {
        "spread": spread_done,
        "back": lambda: send_back(1),
        "fetch": fetch_rest,
        "names": names_done,
        "screen": lambda: loop(0, OCC // JOINED, screen),
    }
    for i in range(blocks):
        steps[f"pair{i}"] = functools.partial(pair_mine, i)
    for t in range(transfers):
        steps[f"far{t}"] = functools.partial(returned, t)
        steps[f"swap{t}"] = functools.partial(exchanged, t)
    for i, lane in enumerate(lanes):
        steps[f"first{i}"] = functools.partial(lane.step, 0)
        steps[f"second{i}"] = functools.partial(lane.step, 1)
        steps[f"middle{i}"] = functools.partial(middle, lane)
        steps[f"turn{i}"] = functools.partial(last_down, lane)
        steps[f"up{i}"] = functools.partial(raise_lane, lane, 1)
        steps[f"rest{i}"] = functools.partial(rest_up, lane)
        steps[f"done{i}"] = functools.partial(lane_done, i)
    for i in range(fetched):
        for level in range(len(SHARE[i]) + 1):
            steps[f"relay{i}{level}"] = functools.partial(relay, i, level)
        steps[f"other{i}"] = functools.partial(pair_other, i)
    total[...] = jnp.zeros_like(total)
    for name in ORDER:
        steps[name]()
    total[...] = 0.5 * total[...]

    def meet(i):
        count = own.shape[2]
        total[...] += gram(
            zbuf[i].reshape(OCC * count, 128), incoming[i].reshape(OCC * count, 128)
        )

    def meet_other(i, carry):
        meet(i)
        return carry

    def meet_sent(i, carry):
        cross_copy(i).wait()
        meet(i)
        return carry

    lax.fori_loop(crossing, blocks, meet_other, 0)
    lax.fori_loop(0, crossing, meet_sent, 0)
    value = total[...]
    bands = value.shape[0] // 2
    real = value[:bands, :bands] + value[bands:, bands:]
    imag = value[:bands, bands:] - value[bands:, :bands]
    sigma = prefactor * jnp.concatenate([real + real.T, imag - imag.T], axis=1)
    top, bottom = sigma[: bands // 2], sigma[bands // 2 :]
    low = half == 0
    give[...] = jnp.where(low, bottom, top)
    last = remote(give, got, sf.at[0], rf.at[0], across)
    last.start()
    mine = jnp.where(low, top, bottom)
    last.wait()
    out_ref[...] = mine + got[...]


def lane_orders(bits):
    order = list(range(bits))
    return [order, [0, 2, 1] + order[3:]]


def local(n, coefficients, triple, neighbors, w_screened, partner, q_ids):
    transfers = partner.shape[0]
    coef = coefficients[0]
    orbitals, doubled = coef.shape
    atoms, neigh, per_atom, width = triple.shape
    size = w_screened.shape[1]
    naux = w_screened.shape[2] // 2
    prefactor = -1.0 / math.sqrt(transfers * naux * OCC)
    bits = n.bit_length() - 1
    blocks = atoms // GROUP
    pairs = orbitals // 128
    bf16 = jnp.bfloat16
    block = (n, pairs * OCC // n, 128)
    sizes = down_rows(n, 2 * size)
    lanes = 2
    cut = size % 256
    fetched = len(SHARE)
    chunk = (blocks, OCC, GROUP * AUX_ATOM, doubled)
    wide = (2 * size, size)
    scratch = [
        VMEM(coef.shape, bf16),
        VMEM((atoms * neigh, per_atom, width), bf16),
        VMEM(w_screened.shape[1:], bf16),
        VMEM(block, bf16),
        VMEM(block, bf16),
        VMEM((transfers,) + block, bf16),
        VMEM((transfers,) + block, bf16),
        VMEM((transfers,) + block, bf16),
        VMEM((2, pairs, 2 * transfers * OCC, 128), bf16),
        [VMEM((size, size), bf16)] * lanes,
        [VMEM((size, size), bf16)] * lanes,
        [[VMEM((rows, size), bf16) for rows in sizes[:-1]]] * lanes,
        [[VMEM((rows, size), bf16) for rows in sizes]] * lanes,
        [VMEM(wide, bf16)] * lanes,
        [VMEM((2 * cut, size), bf16)] * lanes,
        [VMEM((2 * (size - cut), size - cut), bf16)] * lanes,
        VMEM(wide, bf16),
        VMEM(chunk, bf16),
        VMEM(chunk, bf16),
        VMEM(chunk, bf16),
        VMEM(chunk, bf16),
        VMEM((transfers, GROUP * AUX_ATOM * OCC, 128), jnp.float32),
        VMEM((doubled, doubled), jnp.float32),
        VMEM((doubled // 4, doubled), jnp.float32),
        VMEM((doubled // 4, doubled), jnp.float32),
        VMEM((fetched, GROUP * neigh, per_atom, width), bf16),
        VMEM((neigh, atoms), jnp.int32),
        SMEM((neigh, atoms), jnp.int32),
        DMA((4,)),
        DMA((blocks,)),
        DMA((n,)),
        DMA((n,)),
        DMA((transfers, n)),
        DMA((transfers, n)),
        DMA((transfers,)),
        DMA((transfers,)),
        [[DMA((bits,))] * 4] * lanes,
        DMA((blocks,)),
        DMA((blocks,)),
        DMA((2,)),
        DMA((2,)),
        [DMA((fetched,))] * 2 + [DMA((fetched, 3))] * 2,
    ]
    any_spec = pl.BlockSpec(memory_space=pl.ANY)
    smem_spec = pl.BlockSpec(memory_space=SMEM)
    result = pl.pallas_call(
        functools.partial(sigma_kernel, n, prefactor),
        out_shape=jax.ShapeDtypeStruct((doubled // 4, doubled), jnp.float32),
        in_specs=[smem_spec] * 3 + [any_spec] * 4,
        out_specs=pl.BlockSpec(memory_space=VMEM),
        scratch_shapes=scratch,
        compiler_params=pltpu.CompilerParams(collective_id=0, has_side_effects=True),
        name="sigma",
    )(
        partner,
        q_ids,
        neighbors.T,
        neighbors.T,
        coef,
        triple.reshape(atoms * neigh, per_atom, width),
        w_screened[0],
    )
    return result[None]


def solution(mesh):
    in_specs = (
        P("ka", None, None),
        P("aux", None, None, None),
        P("aux", None),
        P("ka", "aux", None),
        P(),
        P(),
    )
    return jax.shard_map(
        functools.partial(local, mesh.shape["ka"]),
        mesh=mesh,
        in_specs=in_specs,
        out_specs=P("ka", "aux", None),
        check_vma=False,
    )
```

```python
import functools
import math

import jax
import jax.numpy as jnp
from jax import lax
from jax.experimental import pallas as pl
from jax.experimental.pallas import tpu as pltpu
from jax.sharding import PartitionSpec as P

AUX_ATOM = 12
OCC = 16
GROUP = 4
JOINED = 4
SHARE = ((1, 2), (2, 1), (1, 2))
EARLY = 3
ORDER = (
    "first0", "first1", "spread", "back", "second0", "second1", "relay00", "far0", "middle1",
    "middle0", "far1", "relay20", "relay10", "swap0", "turn1", "swap1", "pair0", "pair1", "turn0",
    "relay11", "pair2", "pair3", "up1", "up0", "relay01", "pair4", "pair5", "pair6", "pair7",
    "rest1", "rest0", "relay21", "relay12", "relay02", "done1", "done0", "screen", "relay22",
    "names", "other0", "other1", "other2",
)
VMEM = pltpu.VMEM
SMEM = pltpu.SMEM
DMA = pltpu.SemaphoreType.DMA
MESH = pl.DeviceIdType.MESH


def bit_of(me, b):
    return lax.rem(lax.div(me, 1 << b), 2)


def flipped(me, b):
    return me + (1 << b) - 2 * (1 << b) * bit_of(me, b)


def down_rows(n, rows):
    sizes = []
    bits = n.bit_length() - 1
    for b in range(bits):
        rows = rows // 2 if rows // 2 % 16 == 0 and b < bits - 1 else rows
        sizes.append(rows)
    return sizes


class Lane:
    def __init__(self, me, order, sent, kept, full, accs, recvs, sems):
        self.me, self.order = me, order
        self.sent, self.kept, self.full, self.accs, self.recvs = sent, kept, full, accs, recvs
        self.sizes = [x.shape[0] for x in recvs]
        rows = full.shape[0]
        self.halved, self.starts, at = [], [], 0
        for b, size in zip(order, self.sizes):
            self.halved.append(size < rows)
            if size < rows:
                at = at + bit_of(me, b) * size
            self.starts.append(pl.multiple_of(at, 16))
            rows = size
        self.down_send, self.down_recv, self.up_send, self.up_recv = sems

    def peer(self, s):
        return {"ka": flipped(self.me, self.order[s])}

    def down(self, s):
        if s == 0:
            out = self.sent
        elif self.halved[s]:
            away = pl.multiple_of((1 - bit_of(self.me, self.order[s])) * self.sizes[s], 16)
            out = self.accs[s - 1].at[pl.ds(away, self.sizes[s])]
        else:
            out = self.accs[s - 1]
        return remote(out, self.recvs[s], self.down_send.at[s], self.down_recv.at[s], self.peer(s))

    def step(self, s):
        self.down(s).wait()
        if s == 0:
            mine = self.kept[...]
        elif self.halved[s]:
            near = pl.multiple_of(bit_of(self.me, self.order[s]) * self.sizes[s], 16)
            mine = self.accs[s - 1][pl.ds(near, self.sizes[s])]
        else:
            mine = self.accs[s - 1][...]
        summed = mine + self.recvs[s][...]
        if s == len(self.order) - 1:
            self.full[pl.ds(self.starts[s], self.sizes[s])] = summed
        else:
            self.accs[s][...] = summed
            self.down(s + 1).start()

    def up(self, s):
        span = pl.ds(self.starts[s], self.sizes[s])
        return remote(
            self.full.at[span], self.full.at[span], self.up_send.at[s], self.up_recv.at[s], self.peer(s)
        )


def remote(src, dst, send, recv, device):
    return pltpu.make_async_remote_copy(
        src_ref=src, dst_ref=dst, send_sem=send, recv_sem=recv, device_id=device, device_id_type=MESH
    )


def pick_bands(first, coef, src):
    rows = src.shape[1]
    doubled = coef.shape[1]
    high = 2 * OCC
    pairs = src.shape[0] * rows // high
    band = lax.broadcasted_iota(jnp.int32, (high, doubled), 0)
    col = lax.broadcasted_iota(jnp.int32, (high, doubled), 1)
    want = jnp.where(band < OCC, band, band - OCC + doubled // 2)
    choose = jnp.where(col == want, 1.0, 0.0).astype(jnp.bfloat16)
    step = min(8, pairs)
    for p0 in range(0, pairs, step):
        wide = lax.dot_general(
            choose,
            coef[pl.ds(pl.multiple_of(first + p0 * 128, 128), step * 128), :],
            (((1,), (1,)), ((), ())),
            preferred_element_type=jnp.float32,
        ).astype(jnp.bfloat16)
        for p in range(p0, p0 + step):
            block = wide[:, (p - p0) * 128 : (p - p0 + 1) * 128]
            if rows >= high:
                at = p * high % rows
                src[p * high // rows, at : at + high, :] = block
            else:
                for i in range(high // rows):
                    src[p * (high // rows) + i] = block[i * rows : (i + 1) * rows]


def mask_weights(me, half, q_ref, w, kept, sent):
    size = w.shape[0]
    naux = w.shape[1] // 2
    own = pl.multiple_of(half * size, 128)
    other = pl.multiple_of((1 - half) * size, 128)
    first = me == q_ref[half]
    second = me == q_ref[1 - half]
    low = bit_of(me, 0) == 0
    tile = 64
    for r in range(0, size, tile):
        span = slice(r, r + tile)
        row = lax.broadcasted_iota(jnp.int32, (tile, size), 0) + r
        col = lax.broadcasted_iota(jnp.int32, (tile, size), 1)
        packed = jnp.where(
            row <= col,
            w[span, pl.ds(own, size)].astype(jnp.float32),
            w[span, pl.ds(own + naux, size)].astype(jnp.float32),
        ).astype(jnp.bfloat16)
        zero = jnp.zeros_like(packed)
        pieces = [
            jnp.where(first, packed, zero),
            jnp.where(second, packed, zero),
            jnp.where(first, w[span, pl.ds(other, size)], zero),
            jnp.where(first, w[span, pl.ds(other + naux, size)], zero),
        ]
        for i in range(2):
            lower, upper = pieces[2 * i : 2 * i + 2]
            kept[i][span] = jnp.where(low, lower, upper)
            sent[i][span] = jnp.where(low, upper, lower)


def place_far(t, transfers, first, landed, far):
    rows = landed.shape[1]
    high = 2 * OCC
    for p in range(landed.shape[0] * rows // high):
        if rows >= high:
            at = p * high % rows
            block = landed[p * high // rows, at : at + high, :]
        else:
            block = jnp.concatenate(
                [landed[p * (high // rows) + i] for i in range(high // rows)], axis=0
            )
        turned = pltpu.roll(block.astype(jnp.float32), 64, 1).astype(jnp.bfloat16)
        for r in range(2):
            at = pl.multiple_of((r * transfers + t) * OCC, OCC)
            far[0, first + p, pl.ds(at, OCC), :] = block[r * OCC : (r + 1) * OCC]
            far[1, first + p, pl.ds(at, OCC), :] = turned[r * OCC : (r + 1) * OCC]


def pair_group(first_atom, nb_ref, far, triple, coef, outs, stage):
    low = lax.broadcasted_iota(jnp.int32, (4 * OCC, 128), 1) < 64
    sign = jnp.where(lax.broadcasted_iota(jnp.int32, (64, 128), 1) < 64, 1.0, -1.0)
    zero = jnp.zeros((64, 128), jnp.bfloat16)
    for g in range(GROUP):
        n0 = nb_ref(0, g)
        n1 = nb_ref(1, g)
        x0 = far[lax.rem(n0, 2), lax.div(n0, 2)]
        x1 = far[1 - lax.rem(n1, 2), lax.div(n1, 2)]
        lhs = jnp.where(low, x0, x1)
        half = jnp.dot(lhs, triple(g), preferred_element_type=jnp.float32)
        half = half.astype(jnp.bfloat16)
        top, bottom = half[: 2 * OCC], half[2 * OCC :]
        at = pl.multiple_of((first_atom + g) * 64, 64)
        home = coef[pl.ds(at, 64), :].astype(jnp.float32)
        with_real = (home * sign).astype(jnp.bfloat16)
        with_imag = pltpu.roll(home, 64, 1).astype(jnp.bfloat16)
        rhs = jnp.concatenate(
            [
                jnp.concatenate([with_real, zero], axis=1),
                jnp.concatenate([zero, with_real], axis=1),
                jnp.concatenate([with_imag, zero], axis=1),
                jnp.concatenate([zero, with_imag], axis=1),
            ],
            axis=0,
        )
        rows = jnp.concatenate(
            [
                jnp.concatenate(
                    [top[:, s * 128 : (s + 1) * 128], bottom[:, s * 128 : (s + 1) * 128]], axis=1
                )
                for s in range(AUX_ATOM // 2)
            ],
            axis=0,
        )
        prod = jnp.dot(rows, rhs, preferred_element_type=jnp.float32)
        for s in range(AUX_ATOM // 2):
            for t in outs:
                for b in range(2):
                    at = (g * AUX_ATOM + 2 * s + b) * OCC
                    r = s * 2 * OCC + t * OCC
                    stage[t, at : at + OCC, :] = prod[r : r + OCC, b * 128 : (b + 1) * 128]
    count = GROUP * AUX_ATOM
    for t, out in outs.items():
        for l in range(OCC):
            out[l] = stage[t, pl.ds(l, count, stride=OCC), :].astype(jnp.bfloat16)


def unpack_diagonal(packed, upper, lower):
    size = packed.shape[1]
    cut = upper.shape[0] // 2
    row = lax.broadcasted_iota(jnp.int32, (size, size), 0)
    col = lax.broadcasted_iota(jnp.int32, (size, size), 1)
    value = packed.astype(jnp.float32)
    turned = value.T
    real = jnp.where(row <= col, value, turned)
    imag = jnp.where(row > col, value, -turned)
    imag = jnp.where(row == col, 0.0, imag)
    scale = jnp.where(lax.broadcasted_iota(jnp.int32, (cut, size), 1) < cut, 0.5, 1.0)
    upper[:cut] = (scale * real[:cut]).astype(jnp.bfloat16)
    upper[cut:] = (scale * imag[:cut]).astype(jnp.bfloat16)
    lower[: size - cut] = (0.5 * real[cut:, cut:]).astype(jnp.bfloat16)
    lower[size - cut :] = (0.5 * imag[cut:, cut:]).astype(jnp.bfloat16)


def unpack_cross(full, cross):
    size = full.shape[1]
    for i in range(2):
        span = slice(i * size, (i + 1) * size)
        cross[span] = full[span].astype(jnp.float32).T.astype(jnp.bfloat16)


def columns(x, e):
    return [
        jnp.concatenate([x[c, e * JOINED + i] for c in range(x.shape[0])], axis=0)
        for i in range(JOINED)
    ]


def apply(weights, wide, conj):
    size = weights.shape[0] // 2
    sign = jnp.where(lax.broadcasted_iota(jnp.int32, (size, 128), 1) < 64, -1.0, 1.0)
    prod = jnp.dot(weights[...], wide, preferred_element_type=jnp.float32)
    result = []
    for i in range(JOINED):
        re = prod[:size, i * 128 : (i + 1) * 128]
        im = sign * pltpu.roll(prod[size:, i * 128 : (i + 1) * 128], 64, 1)
        result.append((re - im if conj else re + im).astype(jnp.bfloat16))
    return result


def gram(left, right):
    return lax.dot_general(left, right, (((0,), (0,)), ((), ())), preferred_element_type=jnp.float32)


def diagonal(parts, upper, lower):
    cut = upper.shape[0] // 2
    wide = jnp.concatenate(parts, axis=1)
    first = apply(upper, wide, False)
    rest = apply(lower, wide[cut:], False)
    return [part for both in zip(first, rest) for part in both]


def screen_bands(e, own, part, uppers, lowers, cross, zbuf, total):
    count = own.shape[2]
    mine = columns(own, e)
    for i, z in enumerate(apply(cross, jnp.concatenate(mine, axis=1), True)):
        for c in range(own.shape[0]):
            zbuf[c, e * JOINED + i] = z[c * count : (c + 1) * count]
    theirs = columns(part, e)
    screened = diagonal(mine, uppers[0], lowers[0]) + diagonal(theirs, uppers[1], lowers[1])
    total[...] += gram(jnp.concatenate(mine + theirs, axis=0), jnp.concatenate(screened, axis=0))


def sigma_kernel(
    n, prefactor, partner_ref, q_ref, nb_ref, nb_in, coef_in, triple_in, w_in, out_ref,
    coef, triple, w, src, spread, picked, landed, swapped, far,
    kept, sent, accs, recvs, full, uppers, lowers, cross,
    own, part, incoming, zbuf, stage, total, give, got, other, nb_land, nb_other,
    local_sem, triple_sem, s1, r1, s2, r2, s3, r3, lane_sems, sc, rc, sf, rf, fetch_sems,
):
    me = lax.axis_index("ka")
    half = lax.axis_index("aux")
    transfers = partner_ref.shape[0]
    atoms = triple.shape[0] // 2
    group_rows = 2 * GROUP
    blocks = own.shape[0]
    fetched = len(SHARE)
    crossing = blocks - fetched
    bits = n.bit_length() - 1
    across = {"aux": 1 - half}
    barrier = pltpu.get_barrier_semaphore()

    def greet(off, carry):
        dst = lax.rem(me + off, n)
        pl.semaphore_signal(barrier, inc=1, device_id={"ka": dst}, device_id_type=MESH)
        return carry

    lax.fori_loop(1, n, greet, 0)
    pl.semaphore_signal(barrier, inc=1, device_id=across, device_id_type=MESH)

    def get_coef(near):
        rows = coef.shape[0] // 2
        span = pl.ds(pl.multiple_of((half if near else 1 - half) * rows, 128), rows)
        return pltpu.make_async_copy(coef_in.at[span], coef.at[span], local_sem.at[0 if near else 2])

    get_w = pltpu.make_async_copy(w_in, w, local_sem.at[1])
    get_coef(True).start()
    get_w.start()

    def get_triple(i):
        span = pl.ds(i * group_rows, group_rows)
        return pltpu.make_async_copy(triple_in.at[span], triple.at[span], triple_sem.at[i])

    def over_peers(act):
        def body(off, carry):
            act(off, lax.rem(me + off, n))
            return carry

        lax.fori_loop(1, n, body, 0)

    def spread_copy(off, dst):
        return remote(src.at[dst], spread.at[me], s1.at[off], r1.at[off], {"ka": dst})

    def return_copy(t, off, dst):
        return remote(picked.at[t, dst], landed.at[t, me], s2.at[t, off], r2.at[t, off], {"ka": dst})

    core = bit_of(me, 0)
    nb_copy = remote(nb_in, nb_land, sf.at[1], rf.at[1], across)

    def swap(t):
        return remote(landed.at[t], swapped.at[t], s3.at[t], r3.at[t], across)

    def piece(i, level):
        bits_of = SHARE[i] + (0,)
        size = group_rows >> len(bits_of)
        at = 0
        for j in range(level, len(bits_of)):
            at = at + (size << j) * bit_of(me, bits_of[j])
        return at, size << level

    def fetch(i):
        at, size = piece(i, 0)
        return remote(
            triple_in.at[pl.ds((crossing + i) * group_rows + at, size)],
            other.at[i, pl.ds(at, size)],
            fetch_sems[0].at[i],
            fetch_sems[1].at[i],
            across,
        )

    def pass_on(i, level):
        at, size = piece(i, level)
        span = other.at[i, pl.ds(at, size)]
        peer = {"ka": flipped(me, (SHARE[i] + (0,))[level])}
        return remote(span, span, fetch_sems[2].at[i, level], fetch_sems[3].at[i, level], peer)

    def relay(i, level):
        if level == 0:
            fetch(i).wait()
        else:
            pass_on(i, level - 1).wait()
        pass_on(i, level).start()

    lanes = [
        Lane(me, order, sent[i], kept[i], full[i], accs[i], recvs[i], lane_sems[i])
        for i, order in enumerate(lane_orders(bits))
    ]

    tops = [s for s in reversed(range(bits)) if lanes[0].halved[s]]

    def raise_lane(lane, i):
        if i > 0:
            lane.up(tops[i - 1]).wait()
        if i < len(tops):
            lane.up(tops[i]).start()

    def cross_copy(i):
        return remote(part.at[i], incoming.at[i], sc.at[i], rc.at[i], across)

    def pair(i, outs):
        pair_group(
            half * atoms + i * GROUP,
            lambda j, g: nb_ref[j, i * GROUP + g],
            far,
            lambda g: triple[pl.ds((i * GROUP + g) * 2, 2)].reshape(128, triple.shape[2]),
            coef,
            outs,
            stage,
        )

    def pair_mine(i):
        get_triple(i).wait()
        pair(i, {0: own.at[i], 1: part.at[i]})
        if i < crossing:
            cross_copy(i).start()

    def pair_other(i):
        pass_on(i, len(SHARE[i])).wait()
        pair_group(
            (1 - half) * atoms + (crossing + i) * GROUP,
            lambda j, g: nb_other[j, (crossing + i) * GROUP + g],
            far,
            lambda g: other[i, 2 * g : 2 * g + 2].reshape(128, triple.shape[2]),
            coef,
            {0: incoming.at[crossing + i]},
            stage,
        )

    def send_back(t):
        over_peers(lambda off, dst: return_copy(t, off, dst).start())

    get_coef(True).wait()
    pick_bands(half * (coef.shape[0] // 2), coef, src)
    get_w.wait()
    mask_weights(me, half, q_ref, w, kept, sent)
    pl.semaphore_wait(barrier, n)
    over_peers(lambda off, dst: spread_copy(off, dst).start())
    for lane in lanes:
        lane.down(0).start()
    nb_copy.start()
    for i in range(EARLY):
        fetch(i).start()
    spread[me] = src[me]
    get_coef(False).start()
    for i in range(blocks):
        get_triple(i).start()

    def pick(t):
        def body(k, carry):
            picked[t, k] = spread[partner_ref[t, k]]
            return carry

        lax.fori_loop(0, n, body, 0)
        landed[t, me] = picked[t, me]

    def spread_done():
        over_peers(lambda off, dst: spread_copy(off, dst).wait())
        for t in range(transfers):
            pick(t)
            if t == 0:
                send_back(t)

    far_half = far.shape[1] // 2

    def returned(t):
        over_peers(lambda off, dst: return_copy(t, off, dst).wait())
        swap(t).start()
        place_far(lax.rem(half + t, 2), transfers, half * far_half, landed.at[t], far)

    def exchanged(t):
        swap(t).wait()
        place_far(lax.rem(half + t, 2), transfers, (1 - half) * far_half, swapped.at[t], far)

    def fetch_rest():
        for i in range(EARLY, fetched):
            fetch(i).start()

    def middle(lane):
        for s in range(2, bits - 1):
            lane.step(s)

    def last_down(lane):
        lane.step(bits - 1)
        raise_lane(lane, 0)

    def rest_up(lane):
        for i in range(2, len(tops)):
            raise_lane(lane, i)

    def names_done():
        get_coef(False).wait()
        nb_copy.wait()
        move = pltpu.make_async_copy(nb_land, nb_other, local_sem.at[3])
        move.start()
        move.wait()

    def lane_done(i):
        raise_lane(lanes[i], len(tops))
        if i == 0:
            size = cross.shape[1]
            for j in range(2):
                unpack_diagonal(full[0][j * size : (j + 1) * size], uppers[j], lowers[j])
        else:
            unpack_cross(full[1], cross)

    def loop(start, stop, body):
        lax.fori_loop(start, stop, body, 0)

    def screen(e, carry):
        screen_bands(e, own, part, uppers, lowers, cross, zbuf, total)
        return carry

    steps = {
        "spread": spread_done,
        "back": lambda: send_back(1),
        "fetch": fetch_rest,
        "names": names_done,
        "screen": lambda: loop(0, OCC // JOINED, screen),
    }
    for i in range(blocks):
        steps[f"pair{i}"] = functools.partial(pair_mine, i)
    for t in range(transfers):
        steps[f"far{t}"] = functools.partial(returned, t)
        steps[f"swap{t}"] = functools.partial(exchanged, t)
    for i, lane in enumerate(lanes):
        steps[f"first{i}"] = functools.partial(lane.step, 0)
        steps[f"second{i}"] = functools.partial(lane.step, 1)
        steps[f"middle{i}"] = functools.partial(middle, lane)
        steps[f"turn{i}"] = functools.partial(last_down, lane)
        steps[f"up{i}"] = functools.partial(raise_lane, lane, 1)
        steps[f"rest{i}"] = functools.partial(rest_up, lane)
        steps[f"done{i}"] = functools.partial(lane_done, i)
    for i in range(fetched):
        for level in range(len(SHARE[i]) + 1):
            steps[f"relay{i}{level}"] = functools.partial(relay, i, level)
        steps[f"other{i}"] = functools.partial(pair_other, i)
    total[...] = jnp.zeros_like(total)
    for name in ORDER:
        steps[name]()

    def meet(i):
        count = own.shape[2]
        total[...] += gram(
            zbuf[i].reshape(OCC * count, 128), incoming[i].reshape(OCC * count, 128)
        )

    def meet_other(i, carry):
        meet(i)
        return carry

    def meet_sent(i, carry):
        cross_copy(i).wait()
        meet(i)
        return carry

    lax.fori_loop(crossing, blocks, meet_other, 0)
    lax.fori_loop(0, crossing, meet_sent, 0)
    value = total[...]
    bands = value.shape[0] // 2
    real = value[:bands, :bands] + value[bands:, bands:]
    imag = value[:bands, bands:] - value[bands:, :bands]
    sigma = prefactor * jnp.concatenate([real + real.T, imag - imag.T], axis=1)
    top, bottom = sigma[: bands // 2], sigma[bands // 2 :]
    low = half == 0
    give[...] = jnp.where(low, bottom, top)
    last = remote(give, got, sf.at[0], rf.at[0], across)
    last.start()
    mine = jnp.where(low, top, bottom)
    last.wait()
    out_ref[...] = mine + got[...]


def lane_orders(bits):
    order = list(range(bits))
    return [order, [0, 2, 1] + order[3:]]


def local(n, coefficients, triple, neighbors, w_screened, partner, q_ids):
    transfers = partner.shape[0]
    coef = coefficients[0]
    orbitals, doubled = coef.shape
    atoms, neigh, per_atom, width = triple.shape
    size = w_screened.shape[1]
    naux = w_screened.shape[2] // 2
    prefactor = -1.0 / math.sqrt(transfers * naux * OCC)
    bits = n.bit_length() - 1
    blocks = atoms // GROUP
    pairs = orbitals // 128
    bf16 = jnp.bfloat16
    block = (n, pairs * OCC // n, 128)
    sizes = down_rows(n, 2 * size)
    lanes = 2
    cut = size % 256
    fetched = len(SHARE)
    chunk = (blocks, OCC, GROUP * AUX_ATOM, doubled)
    wide = (2 * size, size)
    scratch = [
        VMEM(coef.shape, bf16),
        VMEM((atoms * neigh, per_atom, width), bf16),
        VMEM(w_screened.shape[1:], bf16),
        VMEM(block, bf16),
        VMEM(block, bf16),
        VMEM((transfers,) + block, bf16),
        VMEM((transfers,) + block, bf16),
        VMEM((transfers,) + block, bf16),
        VMEM((2, pairs, 2 * transfers * OCC, 128), bf16),
        [VMEM((size, size), bf16)] * lanes,
        [VMEM((size, size), bf16)] * lanes,
        [[VMEM((rows, size), bf16) for rows in sizes[:-1]]] * lanes,
        [[VMEM((rows, size), bf16) for rows in sizes]] * lanes,
        [VMEM(wide, bf16)] * lanes,
        [VMEM((2 * cut, size), bf16)] * lanes,
        [VMEM((2 * (size - cut), size - cut), bf16)] * lanes,
        VMEM(wide, bf16),
        VMEM(chunk, bf16),
        VMEM(chunk, bf16),
        VMEM(chunk, bf16),
        VMEM(chunk, bf16),
        VMEM((transfers, GROUP * AUX_ATOM * OCC, 128), jnp.float32),
        VMEM((doubled, doubled), jnp.float32),
        VMEM((doubled // 4, doubled), jnp.float32),
        VMEM((doubled // 4, doubled), jnp.float32),
        VMEM((fetched, GROUP * neigh, per_atom, width), bf16),
        VMEM((neigh, atoms), jnp.int32),
        SMEM((neigh, atoms), jnp.int32),
        DMA((4,)),
        DMA((blocks,)),
        DMA((n,)),
        DMA((n,)),
        DMA((transfers, n)),
        DMA((transfers, n)),
        DMA((transfers,)),
        DMA((transfers,)),
        [[DMA((bits,))] * 4] * lanes,
        DMA((blocks,)),
        DMA((blocks,)),
        DMA((2,)),
        DMA((2,)),
        [DMA((fetched,))] * 2 + [DMA((fetched, 3))] * 2,
    ]
    any_spec = pl.BlockSpec(memory_space=pl.ANY)
    smem_spec = pl.BlockSpec(memory_space=SMEM)
    result = pl.pallas_call(
        functools.partial(sigma_kernel, n, prefactor),
        out_shape=jax.ShapeDtypeStruct((doubled // 4, doubled), jnp.float32),
        in_specs=[smem_spec] * 3 + [any_spec] * 4,
        out_specs=pl.BlockSpec(memory_space=VMEM),
        scratch_shapes=scratch,
        compiler_params=pltpu.CompilerParams(collective_id=0, has_side_effects=True),
        name="sigma",
    )(
        partner,
        q_ids,
        neighbors.T,
        neighbors.T,
        coef,
        triple.reshape(atoms * neigh, per_atom, width),
        w_screened[0],
    )
    return result[None]


def solution(mesh):
    in_specs = (
        P("ka", None, None),
        P("aux", None, None, None),
        P("aux", None),
        P("ka", "aux", None),
        P(),
        P(),
    )
    return jax.shard_map(
        functools.partial(local, mesh.shape["ka"]),
        mesh=mesh,
        in_specs=in_specs,
        out_specs=P("ka", "aux", None),
        check_vma=False,
    )
```
